32 devices in a mesh: groups: 2 (over x), shard: 16 (over z, y, core).
Axes of the slice: x: 2, y: 2, z: 4, core: 2. Of those that a mesh axis runs over, the one named last changes fastest.
Arguments:
- embeddings: bfloat16 [16384, 1024], P(('groups', 'shard')), parts along dimension 0, may hold values from -6 to 6
- scales: bfloat16 [16384], P(('groups', 'shard')), parts along dimension 0, may hold values from 0.039794922 to 0.119628906
- cluster: int32 [16384, 1], P(('groups', 'shard')), parts along dimension 0, may hold values from 0 to 15; in each aligned block of 512 rows (0 to 511, 512 to 1023, ...) at most 64 rows name the same one
- pair_listed: int32 [32, 5], P(('groups', 'shard')), parts along dimension 0, may hold values from 0 to 1, as said below
Outputs:
- best: float32 [16384], P(('groups', 'shard')), parts along dimension 0
The draws below stay inside these ranges and needn't reach their ends.
There are 2 independent parts, one for each index of `groups`. The reference program is written for one: setup_inputs(seed, part) draws one part's arguments, and reference() takes and returns one part's arrays. A program takes and returns all parts, laid end to end along the dimension named above; each array names one. Nothing has to cross between parts.
Inputs may be any that keep to these rules, and one draw needn't show every extreme that they name: In each shard's 512 rows at most 64 rows name one sub-cluster, and every sub-cluster is named by some row of the group. `pair_listed`: column 0 is 1 for every a < 15; entries with a + k + 1 >= 16 are 0.
All inputs are finite; a program needn't handle non-finite values.
Results may differ from the reference program's by a relative error of at most 0.0003.
Values may be sent and summed in bfloat16 or wider, within the bound.
A program may use at most 64 MiB of HBM per device.

```python
import math
import jax
import jax.numpy as jnp
import numpy as np
from jax import lax

D = 1024
ROWS_DEV = 512
PARTNERS = 5
SUBC = 16
CAP = 64
SLOTS = 1024
ROWS = 8192
N_SHARD = 16


def draw_pair_listed(key, part):
    coin = jax.random.randint(jax.random.fold_in(key, 17), (SUBC, PARTNERS), 0, 2, dtype=jnp.int32)
    column = jnp.arange(PARTNERS, dtype=jnp.int32)[None, :]
    source = jnp.arange(SUBC, dtype=jnp.int32)[:, None]
    listed = jnp.where(column == 0, 1, coin)
    return jnp.where(source + column + 1 < SUBC, listed, 0).astype(jnp.int32)


def block_scale(stream_key, extent, cuts, smallest, largest):
    loudness, own = 1.0, jax.random.fold_in(stream_key, 6)
    for dim, parts in cuts:
        steps = jnp.exp(jax.random.uniform(jax.random.fold_in(own, dim), (parts,), jnp.float32, smallest / len(cuts), largest / len(cuts)))
        loudness = loudness * jnp.repeat(steps, extent[dim] // parts).reshape([-1 if axis == dim else 1 for axis in range(len(extent))])
    return loudness


def routed_block(stream_key, own, number, rows, amount, top, most, slope):
    ranking = jax.random.permutation(stream_key, amount)
    packed, usual = load_shares(amount, rows * top, most, slope, True), load_shares(amount, rows * top, most, slope, False)
    places = jnp.arange(amount)

    def named(lengths, rotation):
        used = int((lengths > 0).sum())
        fixed = max(1, used // 4)
        moved = fixed + (places - fixed + rotation * (used - fixed)) % max(1, amount - fixed)
        return jnp.zeros((amount,), jnp.int32).at[ranking[jnp.where(places < fixed, places, moved)]].set(jnp.asarray(lengths, jnp.int32))

    lengths = jnp.where(number % 4 == 0, named(packed, number // 4), named(usual, number - number // 4 - 1))
    mixed = jax.random.permutation(jax.random.fold_in(own, 3), amount)
    giver, taker = mixed[0:amount // 2 * 2:2], mixed[1:amount // 2 * 2:2]
    slack = jnp.minimum(lengths[giver] - 1, most - lengths[taker]) // 2
    slack = jnp.where((giver == ranking[0]) | (taker == ranking[0]) | (lengths[taker] == 0), 0, jnp.maximum(slack, 0))
    moved = jax.random.randint(jax.random.fold_in(own, 4), (amount // 2,), 0, 1 << 20) % (slack + 1)
    lengths = lengths.at[giver].add(-moved).at[taker].add(moved)
    items = jnp.searchsorted(jnp.cumsum(lengths), jnp.arange(rows * top), side="right").astype(jnp.int32)
    grid = items.reshape(top, rows).T
    grid = grid[jax.random.permutation(jax.random.fold_in(own, 1), rows)]
    rotation = jax.random.randint(jax.random.fold_in(own, 2), (rows, 1), 0, top)
    return jnp.take_along_axis(grid, (jnp.arange(top)[None, :] + rotation) % top, axis=1)


def load_shares(count, total, most, skew, full):
    portions = [(1 << 20) // math.isqrt(grade ** skew) + 1 for grade in range(1, count + 1)]
    largest = most if full else min(most, max(-(-total // count), total * portions[0] // sum(portions)))
    least = 1 if total - largest >= count - 1 else 0
    counts, spare = [largest] + [least] * (count - 1), total - largest - least * (count - 1)
    while spare > 0:
        free = [i for i in range(1, count) if counts[i] < largest] or [i for i in range(1, count) if counts[i] < most]
        whole, left = sum([portions[i] for i in free]), spare
        for i in free:
            extra = min(most - counts[i], max(1, left * portions[i] // whole), spare)
            counts[i] = counts[i] + extra
            spare = spare - extra
    return np.array(counts)


def gaussian(own_key, dims, width, bound, cuts=(), kind=jnp.bfloat16):
    level = block_scale(own_key, dims, cuts, -0.22, 0.18) if cuts else 1.0
    array = jax.random.normal(own_key, dims, jnp.float32) * width * level
    return jnp.minimum(jnp.maximum(array, -bound), bound).astype(kind)


def setup_inputs(seed: int = 0, part: int = 0) -> dict:
    key_list = jax.random.split(jax.random.key(seed), 5)
    part_splits = jax.random.split(jax.random.fold_in(key_list[4], part), 5)
    embeddings = gaussian(part_splits[0], (ROWS, D), 1.0, 6.0, ((0, 16),))
    scales = jnp.clip(jnp.exp(math.log(0.119628906) - 1.1006552 * jax.random.uniform(part_splits[1], (ROWS,), jnp.float32) ** block_scale(part_splits[1], (ROWS,), ((0, 16),), -0.2, 0.2)), 0.039794922, 0.119628906).astype(jnp.bfloat16)
    cluster_keys = jax.random.split(jax.random.fold_in(part_splits[2], 1), ROWS // ROWS_DEV)
    cluster_turns = jax.random.permutation(jax.random.fold_in(part_splits[2], 3), ROWS // ROWS_DEV)
    cluster = jax.vmap(lambda own, number: routed_block(jax.random.fold_in(part_splits[2], 2), own, number, ROWS_DEV, SUBC, 1, CAP, 2))(cluster_keys, cluster_turns).reshape((ROWS, 1))
    pair_listed = draw_pair_listed(jax.random.fold_in(jax.random.fold_in(key_list[4], part), 71), part)
    return {"embeddings": embeddings, "scales": scales, "cluster": cluster, "pair_listed": pair_listed}


def slot_positions(cluster):
    shard_cluster = cluster.reshape(N_SHARD, ROWS_DEV)
    onehot = (shard_cluster[:, :, None] == jnp.arange(SUBC, dtype=jnp.int32)[None, None, :]).astype(jnp.int32)
    before = jnp.cumsum(onehot, axis=1) - onehot
    within = jnp.sum(before * onehot, axis=2)
    source = jnp.arange(N_SHARD, dtype=jnp.int32)[:, None] * CAP
    return (within + source).reshape(-1).astype(jnp.int32)


def scaled_tile(left, left_scale, right, right_scale):
    raw = lax.dot_general(left, right, (((1,), (1,)), ((), ())), preferred_element_type=jnp.float32)
    return raw * left_scale.astype(jnp.float32)[:, None] * right_scale.astype(jnp.float32)[None, :]


def reference(embeddings, scales, cluster, pair_listed):
    target = cluster[:, 0].astype(jnp.int32)
    position = slot_positions(target)
    blocks = jnp.zeros((SUBC, SLOTS, D), jnp.bfloat16).at[target, position].set(embeddings)
    block_scales = jnp.zeros((SUBC, SLOTS), jnp.bfloat16).at[target, position].set(scales)
    lowest = jnp.float32(-jnp.inf)
    diagonal = jnp.arange(SLOTS, dtype=jnp.int32)[:, None] == jnp.arange(SLOTS, dtype=jnp.int32)[None, :]

    def per_block(index):
        left = blocks[index]
        left_scale = block_scales[index]
        live_left = left_scale != 0
        scores = scaled_tile(left, left_scale, left, left_scale)
        keep = live_left[None, :] & jnp.logical_not(diagonal)
        row_best = jnp.max(jnp.where(keep, scores, lowest), axis=1)
        columns = []
        for step in range(PARTNERS):
            other = index + step + 1
            inside = other < SUBC
            clamped = jnp.minimum(other, SUBC - 1).astype(jnp.int32)
            right = blocks[clamped]
            right_scale = block_scales[clamped]
            listed = (pair_listed[index, step] == 1) & inside
            scores = scaled_tile(left, left_scale, right, right_scale)
            live = listed & live_left[:, None] & (right_scale != 0)[None, :]
            masked = jnp.where(live, scores, lowest)
            row_best = jnp.maximum(row_best, jnp.max(masked, axis=1))
            columns.append(jnp.max(masked, axis=0))
        return row_best, jnp.stack(columns)

    rows_best, cols_best = lax.map(per_block, jnp.arange(SUBC, dtype=jnp.int32))
    slot_best = rows_best
    for step in range(PARTNERS):
        offset = step + 1
        filler = jnp.full((offset, SLOTS), lowest, jnp.float32)
        moved = jnp.concatenate([filler, cols_best[:SUBC - offset, step]], axis=0)
        slot_best = jnp.maximum(slot_best, moved)
    return slot_best[target, position]
```

```python
import functools

import jax
import jax.numpy as jnp
from jax import lax
from jax.experimental import pallas as pl
from jax.experimental.pallas import tpu as pltpu
from jax.sharding import PartitionSpec as P

PARTNERS = 5


lowest = -jnp.inf


def passed_along(value, axis, steps):
    count = lax.axis_size(axis)
    initial, last = (max(0, -steps), min(count, count - steps))
    return lax.ppermute(value, axis, [(source, source + steps) for source in range(initial, last)])


def scaled_tile(left, left_scale, right, right_scale):
    raw = lax.dot_general(left, right, (((1,), (1,)), ((), ())), preferred_element_type=jnp.float32)
    return raw * left_scale.astype(jnp.float32)[:, None] * right_scale.astype(jnp.float32)[None, :]


def partner_tile(left, left_scale, right, right_scale):
    scores = scaled_tile(left, left_scale, right, right_scale)
    live = (left_scale != 0)[:, None] & (right_scale != 0)[None, :]
    masked = jnp.where(live, scores, lowest)
    return (jnp.max(masked, axis=1), jnp.max(masked, axis=0))


def per_device(embeddings, scales, cluster, pair_listed):
    rows, width = embeddings.shape
    owners = lax.axis_size("shard")
    capacity = 2 * rows // owners
    slots = owners * capacity
    here = lax.axis_index("shard")
    target = cluster[:, 0]
    onehot = (target[:, None] == jnp.arange(owners, dtype=jnp.int32)[None, :]).astype(jnp.int32)
    before = jnp.cumsum(onehot, axis=0) - onehot
    position = target * capacity + jnp.sum(before * onehot, axis=1)
    placing = (jnp.arange(slots, dtype=jnp.int32)[:, None] == position[None, :]).astype(
        jnp.bfloat16
    )
    packed = jnp.dot(placing, embeddings, preferred_element_type=jnp.float32).astype(jnp.bfloat16)
    packed_scale = jnp.dot(placing, scales, preferred_element_type=jnp.float32).astype(jnp.bfloat16)
    block, block_scale = (
        lax.all_to_all(
            packed.reshape(owners, capacity, width),
            "shard",
            split_axis=0,
            concat_axis=0,
            tiled=True,
        ),
        lax.all_to_all(
            packed_scale.reshape(owners, capacity), "shard", split_axis=0, concat_axis=0, tiled=True
        ),
    )
    block = block.reshape(slots, width)
    block_scale = block_scale.reshape(slots)
    valid = block_scale != 0
    scores = scaled_tile(block, block_scale, block, block_scale)
    counter = jnp.arange(slots, dtype=jnp.int32)
    keep = valid[None, :] & (counter[:, None] != counter[None, :])
    row_best = jnp.max(jnp.where(keep, scores, lowest), axis=1)
    column_best = []
    carried = (block, block_scale)
    for step in range(PARTNERS):
        carried = passed_along((carried[0], carried[1]), "shard", -1)
        listed = pair_listed[0, step] == 1
        rows_part, cols_part = partner_tile(block, block_scale, carried[0], carried[1])
        rows_part = jnp.where(listed, rows_part, lowest)
        cols_part = jnp.where(listed, cols_part, lowest)
        row_best = jnp.maximum(row_best, rows_part)
        column_best.append(cols_part)
    returned = column_best[PARTNERS - 1]
    for step in range(PARTNERS - 1, -1, -1):
        returned = passed_along(returned, "shard", 1)
        returned = jnp.where(here == 0, lowest, returned)
        if step > 0:
            returned = jnp.maximum(returned, column_best[step - 1])
    slot_best = jnp.where(valid, jnp.maximum(row_best, returned), 0.0)
    homeward = lax.all_to_all(
        slot_best.reshape(owners, capacity), "shard", split_axis=0, concat_axis=0, tiled=True
    )
    return jnp.take(homeward.reshape(slots), position)

REACH = 2
CORES = 2
LANES = 128
SUBLANES = 8
CHUNKS = 4
OUT = -(2.0**100)
MESH = pl.DeviceIdType.MESH

OWN, SIB, NEXT, PREV, PREV_SIB, NEXT2, PREV2 = range(7)
LEFT = {OWN: 0, NEXT: 1, NEXT2: 2}
TO_SIB, TO_NEXT, TO_PREV, TO_PREV_SIB, TO_NEXT2, TO_PREV2 = range(6)


def place(position, core, chips):
    side = position // (chips // 2)
    depth = position * (1 - side) + (chips - 1 - position) * side
    return (depth * 2 + side) * CORES + core


def folded(scores):
    return jnp.max(scores.reshape(scores.shape[0] // SUBLANES, SUBLANES, scores.shape[1]), axis=0)


def pair_kernel(
    owners, x_ref, info_ref, listed_ref, out_ref, emb, info, table, column, barred, across, leave, land,
    own_best, table_sems, emb_sems, info_sems, home_sems, local_sem,
):
    rows, width = x_ref.shape
    chunk = rows // CHUNKS
    chips = owners // CORES
    group = lax.axis_index("groups")
    me = lax.axis_index("shard")
    core = lax.rem(me, CORES)
    chip = me // CORES
    side = lax.rem(chip, 2)
    depth = chip // 2
    position = depth * (1 - side) + (chips - 1 - depth) * side

    def at(step):
        return lax.rem(position + step + chips, chips)

    def flipped(where):
        half = where // (chips // 2)
        return core + half - 2 * core * half

    sibling = place(position, 1 - core, chips)
    following = place(at(1), core, chips)
    preceding = place(at(-1), core, chips)
    crossed = place(at(-1), flipped(at(-1)), chips)

    own_copy = pltpu.make_async_copy(x_ref, emb.at[OWN], local_sem.at[0])
    own_copy.start()
    own_listed = pltpu.make_async_copy(listed_ref, table.at[me], local_sem.at[1])
    own_listed.start()

    barrier = pltpu.get_barrier_semaphore()
    for other in range(1, owners):
        pl.semaphore_signal(
            barrier, inc=1, device_id=(group, lax.rem(me + other, owners)), device_id_type=MESH
        )
    pl.semaphore_wait(barrier, owners - 1)

    started = []

    def send(source, target, sems, index, device):
        copy = pltpu.make_async_remote_copy(
            src_ref=source,
            dst_ref=target,
            send_sem=sems.at[(0, *index)],
            recv_sem=sems.at[(1, *index)],
            device_id=(group, device),
            device_id_type=MESH,
        )
        copy.start()
        started.append(copy)
        return copy

    def part(slot, k):
        return emb.at[slot, pl.ds(k * chunk, chunk), :]

    listed = [
        send(listed_ref, table.at[me], table_sems, (other - 1,), lax.rem(me + other, owners))
        for other in range(1, owners)
    ]
    infos = {
        SIB: send(info_ref, info.at[SIB], info_sems, (SIB,), sibling),
        PREV: send(info_ref, info.at[PREV], info_sems, (PREV,), following),
        NEXT: send(info_ref, info.at[NEXT], info_sems, (NEXT,), preceding),
    }
    parts = {}
    for k in range(CHUNKS):
        mine = x_ref.at[pl.ds(k * chunk, chunk), :]
        parts[PREV, k] = send(mine, part(PREV, k), emb_sems, (PREV, k), following)
        parts[NEXT, k] = send(mine, part(NEXT, k), emb_sems, (NEXT, k), preceding)
        parts[SIB, k] = send(mine, part(SIB, k), emb_sems, (SIB, k), sibling)

    across[...] = jnp.full(across.shape, OUT, jnp.float32)
    leave[...] = jnp.full(leave.shape, OUT, jnp.float32)
    own_best[...] = jnp.full(own_best.shape, OUT, jnp.float32)

    for copy in listed:
        copy.wait_recv()
    own_listed.wait()
    upper = table[:, 0, :owners].astype(jnp.bfloat16)

    def info_of(slot):
        return info_ref if slot == OWN else info.at[slot]

    def as_left(slot):
        wide = info_of(slot)[...].astype(jnp.float32)
        wide = jnp.concatenate([wide, jnp.zeros((LANES - wide.shape[0], rows), jnp.float32)], axis=0)
        column[LEFT[slot]] = wide.T

    def as_right(slot):
        named = info_of(slot)[0:owners, :]
        linked = jnp.dot(upper, named, preferred_element_type=jnp.float32) + lax.dot_general(
            upper, named, (((0,), (0,)), ((), ())), preferred_element_type=jnp.float32
        )
        barred[slot] = jnp.where(linked > 0.5, 0.0, OUT).astype(jnp.bfloat16)

    def meet(left, k, right, first, last, to_right=None, diagonal=False, count=1):
        span = pl.ds(k * chunk, count * chunk)
        cols = pl.ds(first * chunk, (last - first) * chunk)
        about = column[LEFT[left], span, :]
        scores = lax.dot_general(
            emb[left, span, :], emb[right, cols, :], (((1,), (1,)), ((), ())),
            preferred_element_type=jnp.float32,
        )
        scores = scores + jnp.dot(
            about[:, :owners].astype(jnp.bfloat16), barred[right, :, cols],
            preferred_element_type=jnp.float32,
        )
        if diagonal:
            own_row = lax.broadcasted_iota(jnp.int32, scores.shape, 0) + k * chunk
            own_col = lax.broadcasted_iota(jnp.int32, scores.shape, 1) + first * chunk
            scores = jnp.where(own_row == own_col, OUT, scores)
        scale = info_of(right)[pl.ds(owners, 1), cols].astype(jnp.float32)
        by_row = scores * scale
        best = across[LEFT[left], span, :]
        for lane in range(0, scores.shape[1], LANES):
            best = jnp.maximum(best, by_row[:, lane : lane + LANES])
        across[LEFT[left], span, :] = best
        if to_right is not None:
            by_col = folded(scores * about[:, owners : owners + 1])
            to_right[:, cols] = jnp.maximum(to_right[:, cols], by_col)

    def finish_left(left, target):
        for lane in range(0, rows, LANES):
            turned = across[LEFT[left], pl.ds(lane, LANES), :].T
            span = pl.ds(lane, LANES)
            target[:, span] = jnp.maximum(target[:, span], folded(turned))

    homes = {}

    def send_home(which, device):
        homes[which] = send(leave.at[which], land.at[which], home_sems, (which,), device)

    as_left(OWN)
    as_right(OWN)
    own_copy.wait()
    for k in range(CHUNKS):
        meet(OWN, k, OWN, 0, CHUNKS, diagonal=True)
    infos[SIB].wait_recv()
    as_right(SIB)
    for k in range(CHUNKS):
        parts[SIB, k].wait_recv()
    for k in range(CHUNKS):
        meet(OWN, k, SIB, 0, CHUNKS)
    finish_left(OWN, own_best)

    infos[PREV].wait_recv()
    infos[NEXT].wait_recv()
    infos[PREV2] = send(info.at[PREV], info.at[PREV2], info_sems, (PREV2,), following)
    infos[NEXT2] = send(info.at[NEXT], info.at[NEXT2], info_sems, (NEXT2,), crossed)
    infos[PREV_SIB] = send(info.at[PREV], info.at[PREV_SIB], info_sems, (PREV_SIB,), sibling)
    as_left(NEXT)
    as_right(PREV)
    for k in range(CHUNKS):
        parts[PREV, k].wait_recv()
        parts[PREV2, k] = send(part(PREV, k), part(PREV2, k), emb_sems, (PREV2, k), following)
        parts[PREV_SIB, k] = send(part(PREV, k), part(PREV_SIB, k), emb_sems, (PREV_SIB, k), sibling)
        parts[NEXT, k].wait_recv()
        parts[NEXT2, k] = send(part(NEXT, k), part(NEXT2, k), emb_sems, (NEXT2, k), crossed)
        meet(NEXT, k, OWN, 0, CHUNKS, own_best)
        meet(NEXT, k, SIB, 0, CHUNKS, leave.at[TO_SIB])
    send_home(TO_SIB, sibling)
    infos[PREV_SIB].wait_recv()
    as_right(PREV_SIB)
    for k in range(CHUNKS):
        parts[PREV_SIB, k].wait_recv()
    for k in range(CHUNKS):
        meet(NEXT, k, PREV, 0, CHUNKS, leave.at[TO_PREV])
        meet(NEXT, k, PREV_SIB, 0, CHUNKS, leave.at[TO_PREV_SIB])
    finish_left(NEXT, leave.at[TO_NEXT])
    send_home(TO_NEXT, following)

    infos[PREV2].wait_recv()
    infos[NEXT2].wait_recv()
    as_left(NEXT2)
    as_right(PREV2)
    for k in range(CHUNKS):
        parts[NEXT2, k].wait_recv()
        meet(NEXT2, k, PREV, 0, CHUNKS, leave.at[TO_PREV])
        meet(NEXT2, k, PREV_SIB, 0, CHUNKS, leave.at[TO_PREV_SIB])
        if k == CHUNKS - 1:
            send_home(TO_PREV, preceding)
            send_home(TO_PREV_SIB, place(at(-1), 1 - core, chips))
        parts[PREV2, k].wait_recv()
        meet(NEXT2, k, PREV2, 0, k + 1, leave.at[TO_PREV2])
        if k:
            meet(NEXT2, 0, PREV2, k, k + 1, leave.at[TO_PREV2], count=k)
    send_home(TO_PREV2, place(at(-2), core, chips))
    finish_left(NEXT2, leave.at[TO_NEXT2])
    send_home(TO_NEXT2, place(at(2), flipped(position), chips))

    best = own_best[...]
    for which in homes:
        homes[which].wait_recv()
        best = jnp.maximum(best, land[which])
    scale = info_ref[pl.ds(owners, 1), :].astype(jnp.float32)
    out_ref[...] = jnp.max(best, axis=0, keepdims=True) * scale
    for copy in started:
        copy.wait_send()


def all_pairs(embeddings, scales, cluster, pair_listed):
    rows, width = embeddings.shape
    owners = lax.axis_size("shard")
    here = lax.axis_index("shard")
    names = jnp.arange(owners, dtype=jnp.int32)
    depth = -(-(owners + 1) // 16) * 16
    onehot = (names[:, None] == cluster[:, 0][None, :]).astype(jnp.bfloat16)
    info = jnp.concatenate(
        [onehot, scales[None, :], jnp.zeros((depth - owners - 1, rows), jnp.bfloat16)], axis=0
    )
    lanes = jnp.arange(LANES, dtype=jnp.int32)
    ahead = lanes[:, None] == here + 1 + jnp.arange(pair_listed.shape[1], dtype=jnp.int32)[None, :]
    linked = jnp.any(ahead & (pair_listed == 1), axis=1) | (lanes == here)
    listed = jnp.broadcast_to(linked.astype(jnp.float32)[None, :], (SUBLANES, LANES))
    vmem = pl.BlockSpec(memory_space=pltpu.VMEM)
    best = pl.pallas_call(
        functools.partial(pair_kernel, owners),
        out_shape=jax.ShapeDtypeStruct((1, rows), jnp.float32),
        in_specs=[pl.BlockSpec(memory_space=pl.ANY), vmem, vmem],
        out_specs=vmem,
        scratch_shapes=[
            pltpu.VMEM((7, rows, width), jnp.bfloat16),
            pltpu.VMEM((7, depth, rows), jnp.bfloat16),
            pltpu.VMEM((owners, SUBLANES, LANES), jnp.float32),
            pltpu.VMEM((3, rows, LANES), jnp.float32),
            pltpu.VMEM((7, owners, rows), jnp.bfloat16),
            pltpu.VMEM((3, rows, LANES), jnp.float32),
            pltpu.VMEM((6, SUBLANES, rows), jnp.float32),
            pltpu.VMEM((6, SUBLANES, rows), jnp.float32),
            pltpu.VMEM((SUBLANES, rows), jnp.float32),
            pltpu.SemaphoreType.DMA((2, owners - 1)),
            pltpu.SemaphoreType.DMA((2, 7, CHUNKS)),
            pltpu.SemaphoreType.DMA((2, 7)),
            pltpu.SemaphoreType.DMA((2, 6)),
            pltpu.SemaphoreType.DMA((2,)),
        ],
        compiler_params=pltpu.CompilerParams(
            collective_id=0, has_side_effects=True, vmem_limit_bytes=48 * 2**20
        ),
        name="all_pairs",
    )(embeddings, info, listed)
    return best.reshape(rows)


def solution(mesh):
    placed = (
        P(("groups", "shard"), None),
        P(("groups", "shard")),
        P(("groups", "shard"), None),
        P(("groups", "shard"), None),
    )
    owners = mesh.shape["shard"]
    work = all_pairs if owners == 4 * REACH * CORES else per_device
    return jax.shard_map(
        work, mesh=mesh, in_specs=placed, out_specs=P(("groups", "shard")), check_vma=False
    )
```

```python
import functools

import jax
import jax.numpy as jnp
from jax import lax
from jax.experimental import pallas as pl
from jax.experimental.pallas import tpu as pltpu
from jax.sharding import PartitionSpec as P

PARTNERS = 5


lowest = -jnp.inf


def passed_along(value, axis, steps):
    count = lax.axis_size(axis)
    initial, last = (max(0, -steps), min(count, count - steps))
    return lax.ppermute(value, axis, [(source, source + steps) for source in range(initial, last)])


def scaled_tile(left, left_scale, right, right_scale):
    raw = lax.dot_general(left, right, (((1,), (1,)), ((), ())), preferred_element_type=jnp.float32)
    return raw * left_scale.astype(jnp.float32)[:, None] * right_scale.astype(jnp.float32)[None, :]


def partner_tile(left, left_scale, right, right_scale):
    scores = scaled_tile(left, left_scale, right, right_scale)
    live = (left_scale != 0)[:, None] & (right_scale != 0)[None, :]
    masked = jnp.where(live, scores, lowest)
    return (jnp.max(masked, axis=1), jnp.max(masked, axis=0))


def per_device(embeddings, scales, cluster, pair_listed):
    rows, width = embeddings.shape
    owners = lax.axis_size("shard")
    capacity = 2 * rows // owners
    slots = owners * capacity
    here = lax.axis_index("shard")
    target = cluster[:, 0]
    onehot = (target[:, None] == jnp.arange(owners, dtype=jnp.int32)[None, :]).astype(jnp.int32)
    before = jnp.cumsum(onehot, axis=0) - onehot
    position = target * capacity + jnp.sum(before * onehot, axis=1)
    placing = (jnp.arange(slots, dtype=jnp.int32)[:, None] == position[None, :]).astype(
        jnp.bfloat16
    )
    packed = jnp.dot(placing, embeddings, preferred_element_type=jnp.float32).astype(jnp.bfloat16)
    packed_scale = jnp.dot(placing, scales, preferred_element_type=jnp.float32).astype(jnp.bfloat16)
    block, block_scale = (
        lax.all_to_all(
            packed.reshape(owners, capacity, width),
            "shard",
            split_axis=0,
            concat_axis=0,
            tiled=True,
        ),
        lax.all_to_all(
            packed_scale.reshape(owners, capacity), "shard", split_axis=0, concat_axis=0, tiled=True
        ),
    )
    block = block.reshape(slots, width)
    block_scale = block_scale.reshape(slots)
    valid = block_scale != 0
    scores = scaled_tile(block, block_scale, block, block_scale)
    counter = jnp.arange(slots, dtype=jnp.int32)
    keep = valid[None, :] & (counter[:, None] != counter[None, :])
    row_best = jnp.max(jnp.where(keep, scores, lowest), axis=1)
    column_best = []
    carried = (block, block_scale)
    for step in range(PARTNERS):
        carried = passed_along((carried[0], carried[1]), "shard", -1)
        listed = pair_listed[0, step] == 1
        rows_part, cols_part = partner_tile(block, block_scale, carried[0], carried[1])
        rows_part = jnp.where(listed, rows_part, lowest)
        cols_part = jnp.where(listed, cols_part, lowest)
        row_best = jnp.maximum(row_best, rows_part)
        column_best.append(cols_part)
    returned = column_best[PARTNERS - 1]
    for step in range(PARTNERS - 1, -1, -1):
        returned = passed_along(returned, "shard", 1)
        returned = jnp.where(here == 0, lowest, returned)
        if step > 0:
            returned = jnp.maximum(returned, column_best[step - 1])
    slot_best = jnp.where(valid, jnp.maximum(row_best, returned), 0.0)
    homeward = lax.all_to_all(
        slot_best.reshape(owners, capacity), "shard", split_axis=0, concat_axis=0, tiled=True
    )
    return jnp.take(homeward.reshape(slots), position)

REACH = 2
CORES = 2
LANES = 128
SUBLANES = 8
CHUNKS = 4
OUT = -(2.0**100)
MESH = pl.DeviceIdType.MESH

OWN, SIB, NEXT, PREV, PREV_SIB, NEXT2, PREV2 = range(7)
LEFT = {OWN: 0, NEXT: 1, NEXT2: 2}
TO_SIB, TO_NEXT, TO_PREV, TO_PREV_SIB, TO_NEXT2, TO_PREV2 = range(6)


def place(position, core, chips):
    side = position // (chips // 2)
    depth = position * (1 - side) + (chips - 1 - position) * side
    return (depth * 2 + side) * CORES + core


def folded(scores):
    return jnp.max(scores.reshape(scores.shape[0] // SUBLANES, SUBLANES, scores.shape[1]), axis=0)


def pair_kernel(
    owners, x_ref, info_ref, listed_ref, out_ref, emb, info, table, column, barred, across, leave, land,
    own_best, table_sems, emb_sems, info_sems, home_sems, local_sem,
):
    rows, width = x_ref.shape
    chunk = rows // CHUNKS
    chips = owners // CORES
    group = lax.axis_index("groups")
    me = lax.axis_index("shard")
    core = lax.rem(me, CORES)
    chip = me // CORES
    side = lax.rem(chip, 2)
    depth = chip // 2
    position = depth * (1 - side) + (chips - 1 - depth) * side

    def at(step):
        return lax.rem(position + step + chips, chips)

    def flipped(where):
        half = where // (chips // 2)
        return core + half - 2 * core * half

    sibling = place(position, 1 - core, chips)
    following = place(at(1), core, chips)
    preceding = place(at(-1), core, chips)
    crossed = place(at(-1), flipped(at(-1)), chips)

    own_copy = pltpu.make_async_copy(x_ref, emb.at[OWN], local_sem.at[0])
    own_copy.start()
    own_listed = pltpu.make_async_copy(listed_ref, table.at[me], local_sem.at[1])
    own_listed.start()

    barrier = pltpu.get_barrier_semaphore()
    for other in range(1, owners):
        pl.semaphore_signal(
            barrier, inc=1, device_id=(group, lax.rem(me + other, owners)), device_id_type=MESH
        )
    pl.semaphore_wait(barrier, owners - 1)

    started = []

    def send(source, target, sems, index, device):
        copy = pltpu.make_async_remote_copy(
            src_ref=source,
            dst_ref=target,
            send_sem=sems.at[(0, *index)],
            recv_sem=sems.at[(1, *index)],
            device_id=(group, device),
            device_id_type=MESH,
        )
        copy.start()
        started.append(copy)
        return copy

    def part(slot, k):
        return emb.at[slot, pl.ds(k * chunk, chunk), :]

    def send_info(slot, device):
        return send(info_ref, info.at[slot], info_sems, (slot,), device)

    listed = []
    for other in range(1, owners):
        target = lax.rem(me + other, owners)
        listed.append(send(listed_ref, table.at[me], table_sems, (other - 1,), target))
    infos = {
        SIB: send_info(SIB, sibling),
        PREV: send_info(PREV, following),
        NEXT: send_info(NEXT, preceding),
        PREV_SIB: send_info(PREV_SIB, place(at(1), 1 - core, chips)),
        PREV2: send_info(PREV2, place(at(2), core, chips)),
        NEXT2: send_info(NEXT2, place(at(-2), flipped(at(-2)), chips)),
    }
    parts = {}
    for k in range(CHUNKS):
        mine = x_ref.at[pl.ds(k * chunk, chunk), :]
        parts[PREV, k] = send(mine, part(PREV, k), emb_sems, (PREV, k), following)
        parts[NEXT, k] = send(mine, part(NEXT, k), emb_sems, (NEXT, k), preceding)
        parts[SIB, k] = send(mine, part(SIB, k), emb_sems, (SIB, k), sibling)

    across[...] = jnp.full(across.shape, OUT, jnp.float32)
    leave[...] = jnp.full(leave.shape, OUT, jnp.float32)
    own_best[...] = jnp.full(own_best.shape, OUT, jnp.float32)

    for copy in listed:
        copy.wait_recv()
    own_listed.wait()
    upper = table[:, 0, :owners].astype(jnp.bfloat16)

    def info_of(slot):
        return info_ref if slot == OWN else info.at[slot]

    def named_of(slot, names):
        name = lax.broadcasted_iota(jnp.int32, (names, rows), 0).astype(jnp.float32)
        return (info_of(slot)[:, 0:rows] == name).astype(jnp.float32)

    def as_left(slot):
        depth = lax.broadcasted_iota(jnp.int32, (LANES, rows), 0)
        wide = jnp.where(depth == owners, info_of(slot)[:, rows:], named_of(slot, LANES))
        column[LEFT[slot]] = wide.T

    def as_right(slot):
        named = named_of(slot, owners).astype(jnp.bfloat16)
        linked = jnp.dot(upper, named, preferred_element_type=jnp.float32) + lax.dot_general(
            upper, named, (((0,), (0,)), ((), ())), preferred_element_type=jnp.float32
        )
        barred[slot] = jnp.where(linked > 0.5, 0.0, OUT).astype(jnp.bfloat16)

    def meet(left, k, right, first, last, to_right=None, diagonal=False, count=1):
        span = pl.ds(k * chunk, count * chunk)
        cols = pl.ds(first * chunk, (last - first) * chunk)
        about = column[LEFT[left], span, :]
        scores = lax.dot_general(
            emb[left, span, :], emb[right, cols, :], (((1,), (1,)), ((), ())),
            preferred_element_type=jnp.float32,
        )
        scores = scores + jnp.dot(
            about[:, :owners].astype(jnp.bfloat16), barred[right, :, cols],
            preferred_element_type=jnp.float32,
        )
        if diagonal:
            own_row = lax.broadcasted_iota(jnp.int32, scores.shape, 0) + k * chunk
            own_col = lax.broadcasted_iota(jnp.int32, scores.shape, 1) + first * chunk
            scores = jnp.where(own_row == own_col, OUT, scores)
        scale = info_of(right)[:, pl.ds(rows + first * chunk, (last - first) * chunk)]
        by_row = scores * scale
        best = across[LEFT[left], span, :]
        for lane in range(0, scores.shape[1], LANES):
            best = jnp.maximum(best, by_row[:, lane : lane + LANES])
        across[LEFT[left], span, :] = best
        if to_right is not None:
            by_col = folded(scores * about[:, owners : owners + 1])
            to_right[:, cols] = jnp.maximum(to_right[:, cols], by_col)

    def finish_left(left, target):
        for lane in range(0, rows, LANES):
            turned = across[LEFT[left], pl.ds(lane, LANES), :].T
            span = pl.ds(lane, LANES)
            target[:, span] = jnp.maximum(target[:, span], folded(turned))

    homes = {}

    def send_home(which, device):
        homes[which] = send(leave.at[which], land.at[which], home_sems, (which,), device)

    as_left(OWN)
    as_right(OWN)
    own_copy.wait()
    for k in range(CHUNKS):
        meet(OWN, k, OWN, 0, CHUNKS, diagonal=True)
    infos[SIB].wait_recv()
    as_right(SIB)
    for k in range(CHUNKS):
        parts[SIB, k].wait_recv()
    for k in range(CHUNKS):
        meet(OWN, k, SIB, 0, CHUNKS)
    finish_left(OWN, own_best)

    infos[PREV].wait_recv()
    infos[NEXT].wait_recv()
    as_left(NEXT)
    as_right(PREV)
    for k in range(CHUNKS):
        parts[PREV, k].wait_recv()
        parts[PREV2, k] = send(part(PREV, k), part(PREV2, k), emb_sems, (PREV2, k), following)
        parts[PREV_SIB, k] = send(part(PREV, k), part(PREV_SIB, k), emb_sems, (PREV_SIB, k), sibling)
        parts[NEXT, k].wait_recv()
        parts[NEXT2, k] = send(part(NEXT, k), part(NEXT2, k), emb_sems, (NEXT2, k), crossed)
        meet(NEXT, k, OWN, 0, CHUNKS, own_best)
        meet(NEXT, k, SIB, 0, CHUNKS, leave.at[TO_SIB])
    send_home(TO_SIB, sibling)
    infos[PREV_SIB].wait_recv()
    as_right(PREV_SIB)
    for k in range(CHUNKS):
        parts[PREV_SIB, k].wait_recv()
    for k in range(CHUNKS):
        meet(NEXT, k, PREV, 0, CHUNKS, leave.at[TO_PREV])
        meet(NEXT, k, PREV_SIB, 0, CHUNKS, leave.at[TO_PREV_SIB])
    finish_left(NEXT, leave.at[TO_NEXT])
    send_home(TO_NEXT, following)

    infos[PREV2].wait_recv()
    infos[NEXT2].wait_recv()
    as_left(NEXT2)
    as_right(PREV2)
    for k in range(CHUNKS):
        parts[NEXT2, k].wait_recv()
        meet(NEXT2, k, PREV, 0, CHUNKS, leave.at[TO_PREV])
        meet(NEXT2, k, PREV_SIB, 0, CHUNKS, leave.at[TO_PREV_SIB])
        if k == CHUNKS - 1:
            send_home(TO_PREV, preceding)
            send_home(TO_PREV_SIB, place(at(-1), 1 - core, chips))
        parts[PREV2, k].wait_recv()
        meet(NEXT2, k, PREV2, 0, k + 1, leave.at[TO_PREV2])
        if k:
            meet(NEXT2, 0, PREV2, k, k + 1, leave.at[TO_PREV2], count=k)
    send_home(TO_PREV2, place(at(-2), core, chips))
    finish_left(NEXT2, leave.at[TO_NEXT2])
    send_home(TO_NEXT2, place(at(2), flipped(position), chips))

    best = own_best[...]
    for which in homes:
        homes[which].wait_recv()
        best = jnp.maximum(best, land[which])
    scale = info_ref[:, rows:]
    out_ref[...] = jnp.max(best, axis=0, keepdims=True) * scale
    for copy in started:
        copy.wait_send()


def all_pairs(embeddings, scales, cluster, pair_listed):
    rows, width = embeddings.shape
    owners = lax.axis_size("shard")
    here = lax.axis_index("shard")
    info = jnp.concatenate(
        [cluster.reshape(1, rows).astype(jnp.float32), scales.reshape(1, rows).astype(jnp.float32)],
        axis=1,
    )
    lanes = jnp.arange(LANES, dtype=jnp.int32)
    ahead = lanes[:, None] == here + 1 + jnp.arange(pair_listed.shape[1], dtype=jnp.int32)[None, :]
    linked = jnp.any(ahead & (pair_listed == 1), axis=1) | (lanes == here)
    listed = linked.astype(jnp.float32)[None, :]
    vmem = pl.BlockSpec(memory_space=pltpu.VMEM)
    best = pl.pallas_call(
        functools.partial(pair_kernel, owners),
        out_shape=jax.ShapeDtypeStruct((1, rows), jnp.float32),
        in_specs=[pl.BlockSpec(memory_space=pltpu.HBM), vmem, vmem],
        out_specs=vmem,
        scratch_shapes=[
            pltpu.VMEM((7, rows, width), jnp.bfloat16),
            pltpu.VMEM((7, 1, 2 * rows), jnp.float32),
            pltpu.VMEM((owners, 1, LANES), jnp.float32),
            pltpu.VMEM((3, rows, LANES), jnp.float32),
            pltpu.VMEM((7, owners, rows), jnp.bfloat16),
            pltpu.VMEM((3, rows, LANES), jnp.float32),
            pltpu.VMEM((6, SUBLANES, rows), jnp.float32),
            pltpu.VMEM((6, SUBLANES, rows), jnp.float32),
            pltpu.VMEM((SUBLANES, rows), jnp.float32),
            pltpu.SemaphoreType.DMA((2, owners - 1)),
            pltpu.SemaphoreType.DMA((2, 7, CHUNKS)),
            pltpu.SemaphoreType.DMA((2, 7)),
            pltpu.SemaphoreType.DMA((2, 6)),
            pltpu.SemaphoreType.DMA((2,)),
        ],
        compiler_params=pltpu.CompilerParams(
            collective_id=0, has_side_effects=True, vmem_limit_bytes=48 * 2**20
        ),
        name="all_pairs",
    )(embeddings, info, listed)
    return best.reshape(rows)


def solution(mesh):
    placed = (
        P(("groups", "shard"), None),
        P(("groups", "shard")),
        P(("groups", "shard"), None),
        P(("groups", "shard"), None),
    )
    owners = mesh.shape["shard"]
    work = all_pairs if owners == 4 * REACH * CORES else per_device
    return jax.shard_map(
        work, mesh=mesh, in_specs=placed, out_specs=P(("groups", "shard")), check_vma=False
    )
```

```python
import functools

import jax
import jax.numpy as jnp
from jax import lax
from jax.experimental import pallas as pl
from jax.experimental.pallas import tpu as pltpu
from jax.sharding import PartitionSpec as P

PARTNERS = 5


lowest = -jnp.inf


def passed_along(value, axis, steps):
    count = lax.axis_size(axis)
    initial, last = (max(0, -steps), min(count, count - steps))
    return lax.ppermute(value, axis, [(source, source + steps) for source in range(initial, last)])


def scaled_tile(left, left_scale, right, right_scale):
    raw = lax.dot_general(left, right, (((1,), (1,)), ((), ())), preferred_element_type=jnp.float32)
    return raw * left_scale.astype(jnp.float32)[:, None] * right_scale.astype(jnp.float32)[None, :]


def partner_tile(left, left_scale, right, right_scale):
    scores = scaled_tile(left, left_scale, right, right_scale)
    live = (left_scale != 0)[:, None] & (right_scale != 0)[None, :]
    masked = jnp.where(live, scores, lowest)
    return (jnp.max(masked, axis=1), jnp.max(masked, axis=0))


def per_device(embeddings, scales, cluster, pair_listed):
    rows, width = embeddings.shape
    owners = lax.axis_size("shard")
    capacity = 2 * rows // owners
    slots = owners * capacity
    here = lax.axis_index("shard")
    target = cluster[:, 0]
    onehot = (target[:, None] == jnp.arange(owners, dtype=jnp.int32)[None, :]).astype(jnp.int32)
    before = jnp.cumsum(onehot, axis=0) - onehot
    position = target * capacity + jnp.sum(before * onehot, axis=1)
    placing = (jnp.arange(slots, dtype=jnp.int32)[:, None] == position[None, :]).astype(
        jnp.bfloat16
    )
    packed = jnp.dot(placing, embeddings, preferred_element_type=jnp.float32).astype(jnp.bfloat16)
    packed_scale = jnp.dot(placing, scales, preferred_element_type=jnp.float32).astype(jnp.bfloat16)
    block, block_scale = (
        lax.all_to_all(
            packed.reshape(owners, capacity, width),
            "shard",
            split_axis=0,
            concat_axis=0,
            tiled=True,
        ),
        lax.all_to_all(
            packed_scale.reshape(owners, capacity), "shard", split_axis=0, concat_axis=0, tiled=True
        ),
    )
    block = block.reshape(slots, width)
    block_scale = block_scale.reshape(slots)
    valid = block_scale != 0
    scores = scaled_tile(block, block_scale, block, block_scale)
    counter = jnp.arange(slots, dtype=jnp.int32)
    keep = valid[None, :] & (counter[:, None] != counter[None, :])
    row_best = jnp.max(jnp.where(keep, scores, lowest), axis=1)
    column_best = []
    carried = (block, block_scale)
    for step in range(PARTNERS):
        carried = passed_along((carried[0], carried[1]), "shard", -1)
        listed = pair_listed[0, step] == 1
        rows_part, cols_part = partner_tile(block, block_scale, carried[0], carried[1])
        rows_part = jnp.where(listed, rows_part, lowest)
        cols_part = jnp.where(listed, cols_part, lowest)
        row_best = jnp.maximum(row_best, rows_part)
        column_best.append(cols_part)
    returned = column_best[PARTNERS - 1]
    for step in range(PARTNERS - 1, -1, -1):
        returned = passed_along(returned, "shard", 1)
        returned = jnp.where(here == 0, lowest, returned)
        if step > 0:
            returned = jnp.maximum(returned, column_best[step - 1])
    slot_best = jnp.where(valid, jnp.maximum(row_best, returned), 0.0)
    homeward = lax.all_to_all(
        slot_best.reshape(owners, capacity), "shard", split_axis=0, concat_axis=0, tiled=True
    )
    return jnp.take(homeward.reshape(slots), position)

REACH = 2
CORES = 2
LANES = 128
SUBLANES = 8
CHUNKS = 4
OUT = -(2.0**100)
MESH = pl.DeviceIdType.MESH

OWN, SIB, NEXT, PREV, PREV_SIB, NEXT2, PREV2, NEXT_SIB, PREV2_SIB, RUNG = range(10)
LEFT = {OWN: 0, NEXT: 1, NEXT2: 2, PREV2: 3, RUNG: 4}
RELAYED = 1
(
    TO_SIB, TO_NEXT, TO_PREV, TO_PREV_SIB, TO_NEXT2, TO_PREV2, TO_NEXT_SIB, TO_PREV2_SIB, TO_RUNG
) = range(9)


def place(position, core, chips):
    side = position // (chips // 2)
    depth = position * (1 - side) + (chips - 1 - position) * side
    return (depth * 2 + side) * CORES + core


def folded(scores):
    return jnp.max(scores.reshape(scores.shape[0] // SUBLANES, SUBLANES, scores.shape[1]), axis=0)


def pair_kernel(
    owners, x_ref, info_ref, listed_ref, out_ref, emb, info, table, column, barred, across, leave, land,
    lent, own_best, lent_sems, table_sems, emb_sems, info_sems, home_sems, local_sem,
):
    rows, width = x_ref.shape
    chunk = rows // CHUNKS
    chips = owners // CORES
    group = lax.axis_index("groups")
    me = lax.axis_index("shard")
    core = lax.rem(me, CORES)
    chip = me // CORES
    side = lax.rem(chip, 2)
    depth = chip // 2
    position = depth * (1 - side) + (chips - 1 - depth) * side

    def at(step):
        return lax.rem(position + step + chips, chips)

    def is_full(step, whose):
        there = at(step)
        turn = there // (chips // 2)
        down = there * (1 - turn) + (chips - 1 - there) * turn
        return lax.rem(down + whose, 2) == 0

    full, full_next, full_prev = is_full(0, group), is_full(1, group), is_full(-1, group)
    light, light_next, light_prev = is_full(0, group + 1), is_full(1, group + 1), is_full(-1, group + 1)
    on_rung = jnp.where(depth == chips // 4 - group, 1, 0)
    rung_from = on_rung + side == 2
    rung_to = on_rung - side == 1
    opposite = place(chips - 1 - position, core, chips)
    sibling = place(position, 1 - core, chips)
    following = place(at(1), core, chips)
    preceding = place(at(-1), core, chips)

    own_copy = pltpu.make_async_copy(x_ref, emb.at[OWN], local_sem.at[0])
    own_copy.start()
    own_listed = pltpu.make_async_copy(listed_ref, table.at[me], local_sem.at[1])
    own_listed.start()

    barrier = pltpu.get_barrier_semaphore()
    for other in range(1, owners):
        pl.semaphore_signal(
            barrier, inc=1, device_id=(group, lax.rem(me + other, owners)), device_id_type=MESH
        )
    pl.semaphore_signal(barrier, inc=1, device_id=(1 - group, me), device_id_type=MESH)
    pl.semaphore_wait(barrier, owners)

    started = []

    def send(source, target, sems, index, device, only=None, whose=group):
        copy = pltpu.make_async_remote_copy(
            src_ref=source,
            dst_ref=target,
            send_sem=sems.at[(0, *index)],
            recv_sem=sems.at[(1, *index)],
            device_id=(whose, device),
            device_id_type=MESH,
        )
        if only is None:
            copy.start()
        elif only is not False:
            pl.when(only)(copy.start)
        if only is not False:
            started.append((copy, only))
        return copy

    def part(slot, k):
        return emb.at[slot, pl.ds(k * chunk, chunk), :]

    def send_info(slot, device):
        return send(info_ref, info.at[slot], info_sems, (slot,), device)

    listed = []
    for other in range(1, owners):
        target = lax.rem(me + other, owners)
        listed.append(send(listed_ref, table.at[me], table_sems, (other - 1,), target))
    infos = {
        SIB: send_info(SIB, sibling),
        PREV: send_info(PREV, following),
        NEXT: send_info(NEXT, preceding),
        PREV_SIB: send_info(PREV_SIB, place(at(1), 1 - core, chips)),
        PREV2: send_info(PREV2, place(at(2), core, chips)),
        NEXT2: send_info(NEXT2, place(at(-2), core, chips)),
        NEXT_SIB: send_info(NEXT_SIB, place(at(-1), 1 - core, chips)),
        PREV2_SIB: send_info(PREV2_SIB, place(at(2), 1 - core, chips)),
        RUNG: send_info(RUNG, opposite),
    }
    parts = {}
    for k in range(CHUNKS):
        mine = x_ref.at[pl.ds(k * chunk, chunk), :]
        parts[PREV, k] = send(mine, part(PREV, k), emb_sems, (PREV, k), following)
        parts[NEXT, k] = send(mine, part(NEXT, k), emb_sems, (NEXT, k), preceding)
        parts[SIB, k] = send(mine, part(SIB, k), emb_sems, (SIB, k), sibling)
        parts[RUNG, k] = send(mine, part(RUNG, k), emb_sems, (RUNG, k), opposite, rung_from)

    across[...] = jnp.full(across.shape, OUT, jnp.float32)
    leave[...] = jnp.full(leave.shape, OUT, jnp.float32)
    own_best[...] = jnp.full(own_best.shape, OUT, jnp.float32)

    for copy in listed:
        copy.wait_recv()
    own_listed.wait()
    upper = table[:, 0, :owners].astype(jnp.bfloat16)

    def info_of(slot):
        return info_ref if slot == OWN else info.at[slot]

    def named_of(slot, names):
        name = lax.broadcasted_iota(jnp.int32, (names, rows), 0).astype(jnp.float32)
        return (info_of(slot)[:, 0:rows] == name).astype(jnp.float32)

    def as_left(slot):
        depth = lax.broadcasted_iota(jnp.int32, (LANES, rows), 0)
        wide = jnp.where(depth == owners, info_of(slot)[:, rows:], named_of(slot, LANES))
        column[LEFT[slot]] = wide.T

    def as_right(slot):
        named = named_of(slot, owners).astype(jnp.bfloat16)
        linked = jnp.dot(upper, named, preferred_element_type=jnp.float32) + lax.dot_general(
            upper, named, (((0,), (0,)), ((), ())), preferred_element_type=jnp.float32
        )
        barred[slot] = jnp.where(linked > 0.5, 0.0, OUT).astype(jnp.bfloat16)

    def meet(left, k, right, first, last, to_right=None, diagonal=False, count=1):
        span = pl.ds(k * chunk, count * chunk)
        cols = pl.ds(first * chunk, (last - first) * chunk)
        about = column[LEFT[left], span, :]
        scores = lax.dot_general(
            emb[left, span, :], emb[right, cols, :], (((1,), (1,)), ((), ())),
            preferred_element_type=jnp.float32,
        )
        scores = scores + jnp.dot(
            about[:, :owners].astype(jnp.bfloat16), barred[right, :, cols],
            preferred_element_type=jnp.float32,
        )
        if diagonal:
            own_row = lax.broadcasted_iota(jnp.int32, scores.shape, 0) + k * chunk
            own_col = lax.broadcasted_iota(jnp.int32, scores.shape, 1) + first * chunk
            scores = jnp.where(own_row == own_col, OUT, scores)
        scale = info_of(right)[:, pl.ds(rows + first * chunk, (last - first) * chunk)]
        by_row = scores * scale
        best = across[LEFT[left], span, :]
        for lane in range(0, scores.shape[1], LANES):
            best = jnp.maximum(best, by_row[:, lane : lane + LANES])
        across[LEFT[left], span, :] = best
        if to_right is not None:
            by_col = folded(scores * about[:, owners : owners + 1])
            to_right[:, cols] = jnp.maximum(to_right[:, cols], by_col)

    def finish_left(left, target):
        for lane in range(0, rows, LANES):
            turned = across[LEFT[left], pl.ds(lane, LANES), :].T
            span = pl.ds(lane, LANES)
            target[:, span] = jnp.maximum(target[:, span], folded(turned))

    homes = {}

    def send_home(which, device):
        homes[which] = send(leave.at[which], land.at[which], home_sems, (which,), device)

    as_left(OWN)
    as_right(OWN)
    own_copy.wait()
    for k in range(CHUNKS):
        meet(OWN, k, OWN, 0, CHUNKS, diagonal=True)
    infos[SIB].wait_recv()
    as_right(SIB)
    for k in range(CHUNKS):
        parts[SIB, k].wait_recv()
    for k in range(CHUNKS):
        meet(OWN, k, SIB, 0, CHUNKS)
    finish_left(OWN, own_best)

    for slot in (PREV, NEXT, PREV_SIB, PREV2, NEXT2, NEXT_SIB, PREV2_SIB, RUNG):
        infos[slot].wait_recv()
    as_left(NEXT)
    as_right(PREV)
    as_right(PREV_SIB)
    relays = {}

    def pass_on(slot, far, k, device, wanted):
        way = 0 if slot == PREV else 1
        if k < RELAYED:
            relays[0, way, k] = send(
                part(slot, k), lent.at[0, way, k], lent_sems, (0, way, k), me, wanted, 1 - group
            )
            parts[far, k] = send(
                lent.at[1, way, k], part(far, k), emb_sems, (far, k), me, False, 1 - group
            )
        else:
            parts[far, k] = send(part(slot, k), part(far, k), emb_sems, (far, k), device, wanted)

    def relay(first, way, k, wanted, device, whose):
        @pl.when(wanted)
        def _():
            relays[first, way, k].wait_recv()

        if first == 0:
            relays[1, way, k] = send(
                lent.at[0, way, k], lent.at[1, way, k], lent_sems, (1, way, k), device, wanted
            )

    for k in range(CHUNKS):
        parts[PREV, k].wait_recv()
        pass_on(PREV, PREV2, k, following, full_next)
        parts[PREV_SIB, k] = send(part(PREV, k), part(PREV_SIB, k), emb_sems, (PREV_SIB, k), sibling)
        parts[NEXT, k].wait_recv()
        pass_on(NEXT, NEXT2, k, preceding, full_prev)
        parts[NEXT_SIB, k] = send(part(NEXT, k), part(NEXT_SIB, k), emb_sems, (NEXT_SIB, k), sibling)
        if 0 < k <= RELAYED:
            relay(0, 0, k - 1, light_next, following, group)
            relay(0, 1, k - 1, light_prev, preceding, group)
        meet(NEXT, k, OWN, 0, CHUNKS, own_best)
        meet(NEXT, k, SIB, 0, CHUNKS, leave.at[TO_SIB])
    for k in range(CHUNKS):
        parts[PREV_SIB, k].wait_recv()
        parts[NEXT_SIB, k].wait_recv()
    for k in range(CHUNKS):
        meet(NEXT, k, PREV, 0, CHUNKS, leave.at[TO_PREV])
        meet(NEXT, k, PREV_SIB, 0, CHUNKS, leave.at[TO_PREV_SIB])
    finish_left(NEXT, leave.at[TO_NEXT])

    @pl.when(rung_to)
    def _():
        as_left(RUNG)
        for k in range(CHUNKS):
            parts[RUNG, k].wait_recv()
            meet(RUNG, k, OWN, 0, CHUNKS, own_best)
            meet(RUNG, k, SIB, 0, CHUNKS, leave.at[TO_SIB])
        finish_left(RUNG, leave.at[TO_RUNG])

    send_home(TO_SIB, sibling)
    send_home(TO_RUNG, opposite)

    for k in range(RELAYED):
        for way in range(2):
            relay(1, way, k, light, None, None)
            far = NEXT2 if way else PREV2
            pl.when(light)(parts[far, k].start)
            started.append((parts[far, k], light))

    @pl.when(full)
    def _():
        for slot in (NEXT2, PREV2):
            as_left(slot)
        for slot in (NEXT, NEXT_SIB, PREV2, PREV2_SIB):
            as_right(slot)
        shared = []
        for k in (*range(RELAYED, CHUNKS), *range(RELAYED)):
            parts[PREV2, k].wait_recv()
            copy = pltpu.make_async_remote_copy(
                src_ref=part(PREV2, k),
                dst_ref=part(PREV2_SIB, k),
                send_sem=emb_sems.at[0, PREV2_SIB, k],
                recv_sem=emb_sems.at[1, PREV2_SIB, k],
                device_id=(group, sibling),
                device_id_type=MESH,
            )
            copy.start()
            shared.append(copy)
            meet(PREV2, k, NEXT, 0, CHUNKS, leave.at[TO_NEXT])
            meet(PREV2, k, NEXT_SIB, 0, CHUNKS, leave.at[TO_NEXT_SIB])
            parts[NEXT2, k].wait_recv()
            meet(NEXT2, k, PREV, 0, CHUNKS, leave.at[TO_PREV])
            meet(NEXT2, k, PREV_SIB, 0, CHUNKS, leave.at[TO_PREV_SIB])
        for copy in shared:
            copy.wait()
        for k in range(CHUNKS):
            meet(NEXT2, k, PREV2, 0, CHUNKS, leave.at[TO_PREV2])
            meet(NEXT2, k, PREV2_SIB, 0, CHUNKS, leave.at[TO_PREV2_SIB])
        finish_left(NEXT2, leave.at[TO_NEXT2])
        finish_left(PREV2, leave.at[TO_PREV2])

    send_home(TO_NEXT, following)
    send_home(TO_NEXT_SIB, place(at(1), 1 - core, chips))
    send_home(TO_PREV, preceding)
    send_home(TO_PREV_SIB, place(at(-1), 1 - core, chips))
    send_home(TO_NEXT2, place(at(2), core, chips))
    send_home(TO_PREV2, place(at(-2), core, chips))
    send_home(TO_PREV2_SIB, place(at(-2), 1 - core, chips))

    best = own_best[...]
    for which in homes:
        homes[which].wait_recv()
        best = jnp.maximum(best, land[which])
    scale = info_ref[:, rows:]
    out_ref[...] = jnp.max(best, axis=0, keepdims=True) * scale
    for copy, only in started:
        if only is None:
            copy.wait_send()
        else:
            pl.when(only)(copy.wait_send)


def all_pairs(embeddings, scales, cluster, pair_listed):
    rows, width = embeddings.shape
    owners = lax.axis_size("shard")
    here = lax.axis_index("shard")
    info = jnp.concatenate(
        [cluster.reshape(1, rows).astype(jnp.float32), scales.reshape(1, rows).astype(jnp.float32)],
        axis=1,
    )
    lanes = jnp.arange(LANES, dtype=jnp.int32)
    ahead = lanes[:, None] == here + 1 + jnp.arange(pair_listed.shape[1], dtype=jnp.int32)[None, :]
    linked = jnp.any(ahead & (pair_listed == 1), axis=1) | (lanes == here)
    listed = linked.astype(jnp.float32)[None, :]
    vmem = pl.BlockSpec(memory_space=pltpu.VMEM)
    best = pl.pallas_call(
        functools.partial(pair_kernel, owners),
        out_shape=jax.ShapeDtypeStruct((1, rows), jnp.float32),
        in_specs=[pl.BlockSpec(memory_space=pltpu.HBM), vmem, vmem],
        out_specs=vmem,
        scratch_shapes=[
            pltpu.VMEM((10, rows, width), jnp.bfloat16),
            pltpu.VMEM((10, 1, 2 * rows), jnp.float32),
            pltpu.VMEM((owners, 1, LANES), jnp.float32),
            pltpu.VMEM((5, rows, LANES), jnp.float32),
            pltpu.VMEM((10, owners, rows), jnp.bfloat16),
            pltpu.VMEM((5, rows, LANES), jnp.float32),
            pltpu.VMEM((9, SUBLANES, rows), jnp.float32),
            pltpu.VMEM((9, SUBLANES, rows), jnp.float32),
            pltpu.VMEM((2, 2, RELAYED, rows // CHUNKS, width), jnp.bfloat16),
            pltpu.VMEM((SUBLANES, rows), jnp.float32),
            pltpu.SemaphoreType.DMA((2, 2, 2, RELAYED)),
            pltpu.SemaphoreType.DMA((2, owners - 1)),
            pltpu.SemaphoreType.DMA((2, 10, CHUNKS)),
            pltpu.SemaphoreType.DMA((2, 10)),
            pltpu.SemaphoreType.DMA((2, 9)),
            pltpu.SemaphoreType.DMA((2,)),
        ],
        compiler_params=pltpu.CompilerParams(
            collective_id=0, has_side_effects=True, vmem_limit_bytes=48 * 2**20
        ),
        name="all_pairs",
    )(embeddings, info, listed)
    return best.reshape(rows)


def solution(mesh):
    placed = (
        P(("groups", "shard"), None),
        P(("groups", "shard")),
        P(("groups", "shard"), None),
        P(("groups", "shard"), None),
    )
    owners = mesh.shape["shard"]
    work = all_pairs if owners == 4 * REACH * CORES and mesh.shape["groups"] == 2 else per_device
    return jax.shard_map(
        work, mesh=mesh, in_specs=placed, out_specs=P(("groups", "shard")), check_vma=False
    )
```

```python
import functools

import jax
import jax.numpy as jnp
from jax import lax
from jax.experimental import pallas as pl
from jax.experimental.pallas import tpu as pltpu
from jax.sharding import PartitionSpec as P

PARTNERS = 5


lowest = -jnp.inf


def passed_along(value, axis, steps):
    count = lax.axis_size(axis)
    initial, last = (max(0, -steps), min(count, count - steps))
    return lax.ppermute(value, axis, [(source, source + steps) for source in range(initial, last)])


def scaled_tile(left, left_scale, right, right_scale):
    raw = lax.dot_general(left, right, (((1,), (1,)), ((), ())), preferred_element_type=jnp.float32)
    return raw * left_scale.astype(jnp.float32)[:, None] * right_scale.astype(jnp.float32)[None, :]


def partner_tile(left, left_scale, right, right_scale):
    scores = scaled_tile(left, left_scale, right, right_scale)
    live = (left_scale != 0)[:, None] & (right_scale != 0)[None, :]
    masked = jnp.where(live, scores, lowest)
    return (jnp.max(masked, axis=1), jnp.max(masked, axis=0))


def per_device(embeddings, scales, cluster, pair_listed):
    rows, width = embeddings.shape
    owners = lax.axis_size("shard")
    capacity = 2 * rows // owners
    slots = owners * capacity
    here = lax.axis_index("shard")
    target = cluster[:, 0]
    onehot = (target[:, None] == jnp.arange(owners, dtype=jnp.int32)[None, :]).astype(jnp.int32)
    before = jnp.cumsum(onehot, axis=0) - onehot
    position = target * capacity + jnp.sum(before * onehot, axis=1)
    placing = (jnp.arange(slots, dtype=jnp.int32)[:, None] == position[None, :]).astype(
        jnp.bfloat16
    )
    packed = jnp.dot(placing, embeddings, preferred_element_type=jnp.float32).astype(jnp.bfloat16)
    packed_scale = jnp.dot(placing, scales, preferred_element_type=jnp.float32).astype(jnp.bfloat16)
    block, block_scale = (
        lax.all_to_all(
            packed.reshape(owners, capacity, width),
            "shard",
            split_axis=0,
            concat_axis=0,
            tiled=True,
        ),
        lax.all_to_all(
            packed_scale.reshape(owners, capacity), "shard", split_axis=0, concat_axis=0, tiled=True
        ),
    )
    block = block.reshape(slots, width)
    block_scale = block_scale.reshape(slots)
    valid = block_scale != 0
    scores = scaled_tile(block, block_scale, block, block_scale)
    counter = jnp.arange(slots, dtype=jnp.int32)
    keep = valid[None, :] & (counter[:, None] != counter[None, :])
    row_best = jnp.max(jnp.where(keep, scores, lowest), axis=1)
    column_best = []
    carried = (block, block_scale)
    for step in range(PARTNERS):
        carried = passed_along((carried[0], carried[1]), "shard", -1)
        listed = pair_listed[0, step] == 1
        rows_part, cols_part = partner_tile(block, block_scale, carried[0], carried[1])
        rows_part = jnp.where(listed, rows_part, lowest)
        cols_part = jnp.where(listed, cols_part, lowest)
        row_best = jnp.maximum(row_best, rows_part)
        column_best.append(cols_part)
    returned = column_best[PARTNERS - 1]
    for step in range(PARTNERS - 1, -1, -1):
        returned = passed_along(returned, "shard", 1)
        returned = jnp.where(here == 0, lowest, returned)
        if step > 0:
            returned = jnp.maximum(returned, column_best[step - 1])
    slot_best = jnp.where(valid, jnp.maximum(row_best, returned), 0.0)
    homeward = lax.all_to_all(
        slot_best.reshape(owners, capacity), "shard", split_axis=0, concat_axis=0, tiled=True
    )
    return jnp.take(homeward.reshape(slots), position)

REACH = 2
CORES = 2
LANES = 128
SUBLANES = 8
CHUNKS = 4
OUT = -(2.0**100)
MESH = pl.DeviceIdType.MESH

OWN, SIB, NEXT, PREV, PREV_SIB, NEXT2, PREV2, NEXT_SIB, PREV2_SIB, RUNG = range(10)
LEFT = {OWN: 0, NEXT: 1, NEXT2: 2, PREV2: 3, RUNG: 4}
RELAYED = 1
(
    TO_SIB, TO_NEXT, TO_PREV, TO_PREV_SIB, TO_NEXT2, TO_PREV2, TO_NEXT_SIB, TO_PREV2_SIB, TO_RUNG
) = range(9)


def place(position, core, chips):
    side = position // (chips // 2)
    depth = position * (1 - side) + (chips - 1 - position) * side
    return (depth * 2 + side) * CORES + core


def folded(scores):
    return jnp.max(scores.reshape(scores.shape[0] // SUBLANES, SUBLANES, scores.shape[1]), axis=0)


def pair_kernel(
    owners, x_ref, info_ref, listed_ref, out_ref, emb, info, table, column, barred, across, leave, land,
    lent, own_best, lent_sems, table_sems, emb_sems, info_sems, home_sems, local_sem,
):
    rows, width = x_ref.shape
    chunk = rows // CHUNKS
    chips = owners // CORES
    group = lax.axis_index("groups")
    me = lax.axis_index("shard")
    core = lax.rem(me, CORES)
    chip = me // CORES
    side = lax.rem(chip, 2)
    depth = chip // 2
    position = depth * (1 - side) + (chips - 1 - depth) * side

    def at(step):
        return lax.rem(position + step + chips, chips)

    def is_full(step, whose):
        there = at(step)
        turn = there // (chips // 2)
        down = there * (1 - turn) + (chips - 1 - there) * turn
        return lax.rem(down + whose, 2) == 0

    full, full_next, full_prev = is_full(0, group), is_full(1, group), is_full(-1, group)
    light, light_next, light_prev = is_full(0, group + 1), is_full(1, group + 1), is_full(-1, group + 1)
    on_rung = jnp.where(depth == chips // 4 - group, 1, 0)
    rung_from = on_rung + side == 2
    rung_to = on_rung - side == 1
    opposite = place(chips - 1 - position, core, chips)
    sibling = place(position, 1 - core, chips)
    following = place(at(1), core, chips)
    preceding = place(at(-1), core, chips)

    own_copy = pltpu.make_async_copy(x_ref, emb.at[OWN], local_sem.at[0])
    own_copy.start()
    own_listed = pltpu.make_async_copy(listed_ref, table.at[me], local_sem.at[1])
    own_listed.start()

    barrier = pltpu.get_barrier_semaphore()
    for other in range(1, owners):
        pl.semaphore_signal(
            barrier, inc=1, device_id=(group, lax.rem(me + other, owners)), device_id_type=MESH
        )
    pl.semaphore_signal(barrier, inc=1, device_id=(1 - group, me), device_id_type=MESH)
    pl.semaphore_wait(barrier, owners)

    started = []

    def send(source, target, sems, index, device, only=None, whose=group):
        copy = pltpu.make_async_remote_copy(
            src_ref=source,
            dst_ref=target,
            send_sem=sems.at[(0, *index)],
            recv_sem=sems.at[(1, *index)],
            device_id=(whose, device),
            device_id_type=MESH,
        )
        if only is None:
            copy.start()
        elif only is not False:
            pl.when(only)(copy.start)
        if only is not False:
            started.append((copy, only))
        return copy

    def part(slot, k):
        return emb.at[slot, pl.ds(k * chunk, chunk), :]

    def send_info(slot, device):
        return send(info_ref, info.at[slot], info_sems, (slot,), device)

    listed = []
    for other in range(1, owners):
        target = lax.rem(me + other, owners)
        listed.append(send(listed_ref, table.at[me], table_sems, (other - 1,), target))
    infos = {
        SIB: send_info(SIB, sibling),
        PREV: send_info(PREV, following),
        NEXT: send_info(NEXT, preceding),
        PREV_SIB: send_info(PREV_SIB, place(at(1), 1 - core, chips)),
        PREV2: send_info(PREV2, place(at(2), core, chips)),
        NEXT2: send_info(NEXT2, place(at(-2), core, chips)),
        NEXT_SIB: send_info(NEXT_SIB, place(at(-1), 1 - core, chips)),
        PREV2_SIB: send_info(PREV2_SIB, place(at(2), 1 - core, chips)),
        RUNG: send_info(RUNG, opposite),
    }
    parts = {}
    for k in range(CHUNKS):
        mine = x_ref.at[pl.ds(k * chunk, chunk), :]
        parts[PREV, k] = send(mine, part(PREV, k), emb_sems, (PREV, k), following)
        parts[NEXT, k] = send(mine, part(NEXT, k), emb_sems, (NEXT, k), preceding)
        parts[SIB, k] = send(mine, part(SIB, k), emb_sems, (SIB, k), sibling)
        parts[RUNG, k] = send(mine, part(RUNG, k), emb_sems, (RUNG, k), opposite, rung_from)

    across[...] = jnp.full(across.shape, OUT, jnp.float32)
    leave[...] = jnp.full(leave.shape, OUT, jnp.float32)
    own_best[...] = jnp.full(own_best.shape, OUT, jnp.float32)

    for copy in listed:
        copy.wait_recv()
    own_listed.wait()
    upper = table[:, 0, :owners].astype(jnp.bfloat16)

    def info_of(slot):
        return info_ref if slot == OWN else info.at[slot]

    def named_of(slot, names):
        name = lax.broadcasted_iota(jnp.int32, (names, rows), 0).astype(jnp.float32)
        return (info_of(slot)[:, 0:rows] == name).astype(jnp.float32)

    def as_left(slot):
        depth = lax.broadcasted_iota(jnp.int32, (LANES, rows), 0)
        wide = jnp.where(depth == owners, info_of(slot)[:, rows:], named_of(slot, LANES))
        column[LEFT[slot]] = wide.T

    def as_right(slot):
        named = named_of(slot, owners).astype(jnp.bfloat16)
        linked = jnp.dot(upper, named, preferred_element_type=jnp.float32) + lax.dot_general(
            upper, named, (((0,), (0,)), ((), ())), preferred_element_type=jnp.float32
        )
        barred[slot] = jnp.where(linked > 0.5, 0.0, OUT).astype(jnp.bfloat16)

    def meet(left, k, right, first, last, to_right=None, diagonal=False, count=1):
        span = pl.ds(k * chunk, count * chunk)
        cols = pl.ds(first * chunk, (last - first) * chunk)
        about = column[LEFT[left], span, :]
        scores = lax.dot_general(
            emb[left, span, :], emb[right, cols, :], (((1,), (1,)), ((), ())),
            preferred_element_type=jnp.float32,
        )
        scores = scores + jnp.dot(
            about[:, :owners].astype(jnp.bfloat16), barred[right, :, cols],
            preferred_element_type=jnp.float32,
        )
        if diagonal:
            own_row = lax.broadcasted_iota(jnp.int32, scores.shape, 0) + k * chunk
            own_col = lax.broadcasted_iota(jnp.int32, scores.shape, 1) + first * chunk
            scores = jnp.where(own_row == own_col, OUT, scores)
        scale = info_of(right)[:, pl.ds(rows + first * chunk, (last - first) * chunk)]
        by_row = scores * scale
        best = across[LEFT[left], span, :]
        for lane in range(0, scores.shape[1], LANES):
            best = jnp.maximum(best, by_row[:, lane : lane + LANES])
        across[LEFT[left], span, :] = best
        if to_right is not None:
            by_col = folded(scores * about[:, owners : owners + 1])
            to_right[:, cols] = jnp.maximum(to_right[:, cols], by_col)

    def finish_left(left, target):
        for lane in range(0, rows, LANES):
            turned = across[LEFT[left], pl.ds(lane, LANES), :].T
            span = pl.ds(lane, LANES)
            target[:, span] = jnp.maximum(target[:, span], folded(turned))

    homes = {}

    def send_home(which, device):
        homes[which] = send(leave.at[which], land.at[which], home_sems, (which,), device)

    as_left(OWN)
    as_right(OWN)
    own_copy.wait()
    for k in range(CHUNKS):
        meet(OWN, k, OWN, 0, CHUNKS, diagonal=True)
    infos[SIB].wait_recv()
    as_right(SIB)
    for k in range(CHUNKS):
        parts[SIB, k].wait_recv()
    for k in range(CHUNKS):
        meet(OWN, k, SIB, 0, CHUNKS)
    finish_left(OWN, own_best)

    for slot in (PREV, NEXT, PREV_SIB, PREV2, NEXT2, NEXT_SIB, PREV2_SIB, RUNG):
        infos[slot].wait_recv()
    as_left(NEXT)
    as_right(PREV)
    as_right(PREV_SIB)
    relays = {}

    def pass_on(slot, far, k, device, wanted):
        way = 0 if slot == PREV else 1
        if k < RELAYED:
            relays[0, way, k] = send(
                part(slot, k), lent.at[0, way, k], lent_sems, (0, way, k), me, wanted, 1 - group
            )
            parts[far, k] = send(
                lent.at[1, way, k], part(far, k), emb_sems, (far, k), me, False, 1 - group
            )
        else:
            parts[far, k] = send(part(slot, k), part(far, k), emb_sems, (far, k), device, wanted)

    def relay(first, way, k, wanted, device, whose):
        @pl.when(wanted)
        def _():
            relays[first, way, k].wait_recv()

        if first == 0:
            relays[1, way, k] = send(
                lent.at[0, way, k], lent.at[1, way, k], lent_sems, (1, way, k), device, wanted
            )

    for k in range(CHUNKS):
        parts[PREV, k].wait_recv()
        pass_on(PREV, PREV2, k, following, full_next)
        parts[PREV_SIB, k] = send(part(PREV, k), part(PREV_SIB, k), emb_sems, (PREV_SIB, k), sibling)
        parts[NEXT, k].wait_recv()
        pass_on(NEXT, NEXT2, k, preceding, full_prev)
        parts[NEXT_SIB, k] = send(part(NEXT, k), part(NEXT_SIB, k), emb_sems, (NEXT_SIB, k), sibling)
        if 0 < k <= RELAYED:
            relay(0, 0, k - 1, light_next, following, group)
            relay(0, 1, k - 1, light_prev, preceding, group)
        meet(NEXT, k, OWN, 0, CHUNKS, own_best)
        meet(NEXT, k, SIB, 0, CHUNKS, leave.at[TO_SIB])
    for k in range(CHUNKS):
        parts[PREV_SIB, k].wait_recv()
        parts[NEXT_SIB, k].wait_recv()
    for k in range(CHUNKS):
        meet(NEXT, k, PREV, 0, CHUNKS, leave.at[TO_PREV])
        meet(NEXT, k, PREV_SIB, 0, CHUNKS, leave.at[TO_PREV_SIB])
    finish_left(NEXT, leave.at[TO_NEXT])

    @pl.when(rung_to)
    def _():
        as_left(RUNG)
        for k in range(CHUNKS):
            parts[RUNG, k].wait_recv()
            meet(RUNG, k, OWN, 0, CHUNKS, own_best)
            meet(RUNG, k, SIB, 0, CHUNKS, leave.at[TO_SIB])
        finish_left(RUNG, leave.at[TO_RUNG])

    send_home(TO_SIB, sibling)
    send_home(TO_RUNG, opposite)

    for k in range(RELAYED):
        for way in range(2):
            relay(1, way, k, light, None, None)
            far = NEXT2 if way else PREV2
            pl.when(light)(parts[far, k].start)
            started.append((parts[far, k], light))

    @pl.when(full)
    def _():
        for slot in (NEXT2, PREV2):
            as_left(slot)
        for slot in (NEXT, NEXT_SIB, PREV2, PREV2_SIB):
            as_right(slot)
        seen = []
        for k in (*range(RELAYED, CHUNKS), *range(RELAYED)):
            parts[PREV2, k].wait_recv()
            copy = pltpu.make_async_remote_copy(
                src_ref=part(PREV2, k),
                dst_ref=part(PREV2_SIB, k),
                send_sem=emb_sems.at[0, PREV2_SIB, k],
                recv_sem=emb_sems.at[1, PREV2_SIB, k],
                device_id=(group, sibling),
                device_id_type=MESH,
            )
            copy.start()
            meet(PREV2, k, NEXT, 0, CHUNKS, leave.at[TO_NEXT])
            meet(PREV2, k, NEXT_SIB, 0, CHUNKS, leave.at[TO_NEXT_SIB])
            parts[NEXT2, k].wait_recv()
            meet(NEXT2, k, PREV, 0, CHUNKS, leave.at[TO_PREV])
            meet(NEXT2, k, PREV_SIB, 0, CHUNKS, leave.at[TO_PREV_SIB])
            copy.wait()
            for j in seen:
                for right, home in ((PREV2, TO_PREV2), (PREV2_SIB, TO_PREV2_SIB)):
                    meet(NEXT2, k, right, j, j + 1, leave.at[home])
                    meet(NEXT2, j, right, k, k + 1, leave.at[home])
            for right, home in ((PREV2, TO_PREV2), (PREV2_SIB, TO_PREV2_SIB)):
                meet(NEXT2, k, right, k, k + 1, leave.at[home])
            seen.append(k)
        finish_left(NEXT2, leave.at[TO_NEXT2])
        finish_left(PREV2, leave.at[TO_PREV2])

    send_home(TO_NEXT, following)
    send_home(TO_NEXT_SIB, place(at(1), 1 - core, chips))
    send_home(TO_PREV, preceding)
    send_home(TO_PREV_SIB, place(at(-1), 1 - core, chips))
    send_home(TO_NEXT2, place(at(2), core, chips))
    send_home(TO_PREV2, place(at(-2), core, chips))
    send_home(TO_PREV2_SIB, place(at(-2), 1 - core, chips))

    best = own_best[...]
    for which in homes:
        homes[which].wait_recv()
        best = jnp.maximum(best, land[which])
    scale = info_ref[:, rows:]
    out_ref[...] = jnp.max(best, axis=0, keepdims=True) * scale
    for copy, only in started:
        if only is None:
            copy.wait_send()
        else:
            pl.when(only)(copy.wait_send)


def all_pairs(embeddings, scales, cluster, pair_listed):
    rows, width = embeddings.shape
    owners = lax.axis_size("shard")
    here = lax.axis_index("shard")
    info = jnp.concatenate(
        [cluster.reshape(1, rows).astype(jnp.float32), scales.reshape(1, rows).astype(jnp.float32)],
        axis=1,
    )
    lanes = jnp.arange(LANES, dtype=jnp.int32)
    ahead = lanes[:, None] == here + 1 + jnp.arange(pair_listed.shape[1], dtype=jnp.int32)[None, :]
    linked = jnp.any(ahead & (pair_listed == 1), axis=1) | (lanes == here)
    listed = linked.astype(jnp.float32)[None, :]
    vmem = pl.BlockSpec(memory_space=pltpu.VMEM)
    best = pl.pallas_call(
        functools.partial(pair_kernel, owners),
        out_shape=jax.ShapeDtypeStruct((1, rows), jnp.float32),
        in_specs=[pl.BlockSpec(memory_space=pltpu.HBM), vmem, vmem],
        out_specs=vmem,
        scratch_shapes=[
            pltpu.VMEM((10, rows, width), jnp.bfloat16),
            pltpu.VMEM((10, 1, 2 * rows), jnp.float32),
            pltpu.VMEM((owners, 1, LANES), jnp.float32),
            pltpu.VMEM((5, rows, LANES), jnp.float32),
            pltpu.VMEM((10, owners, rows), jnp.bfloat16),
            pltpu.VMEM((5, rows, LANES), jnp.float32),
            pltpu.VMEM((9, SUBLANES, rows), jnp.float32),
            pltpu.VMEM((9, SUBLANES, rows), jnp.float32),
            pltpu.VMEM((2, 2, RELAYED, rows // CHUNKS, width), jnp.bfloat16),
            pltpu.VMEM((SUBLANES, rows), jnp.float32),
            pltpu.SemaphoreType.DMA((2, 2, 2, RELAYED)),
            pltpu.SemaphoreType.DMA((2, owners - 1)),
            pltpu.SemaphoreType.DMA((2, 10, CHUNKS)),
            pltpu.SemaphoreType.DMA((2, 10)),
            pltpu.SemaphoreType.DMA((2, 9)),
            pltpu.SemaphoreType.DMA((2,)),
        ],
        compiler_params=pltpu.CompilerParams(
            collective_id=0, has_side_effects=True, vmem_limit_bytes=48 * 2**20
        ),
        name="all_pairs",
    )(embeddings, info, listed)
    return best.reshape(rows)


def solution(mesh):
    placed = (
        P(("groups", "shard"), None),
        P(("groups", "shard")),
        P(("groups", "shard"), None),
        P(("groups", "shard"), None),
    )
    owners = mesh.shape["shard"]
    work = all_pairs if owners == 4 * REACH * CORES and mesh.shape["groups"] == 2 else per_device
    return jax.shard_map(
        work, mesh=mesh, in_specs=placed, out_specs=P(("groups", "shard")), check_vma=False
    )
```
